32 devices in a mesh: tok: 16 (over z, y, x), head: 2 (over core).
Axes of the slice: x: 2, y: 2, z: 4, core: 2. Of those that a mesh axis runs over, the one named last changes fastest.
Arguments:
- queries: bfloat16 [2, 4096, 512], P('head', 'tok'), may hold values from -6 to 6
- key_rows: bfloat16 [2, 4096, 512], P('head', 'tok'), may hold values from -6 to 6
- value_rows: bfloat16 [2, 4096, 512], P('head', 'tok'), may hold values from -6 to 6
- step_rates: float32 [2, 4096], P('head', 'tok'), may hold values from 0.1 to 1
- w_gate: bfloat16 [2, 512, 512], P('head'), may hold values from -0.25 to 0.25
- w_up: bfloat16 [2, 512, 512], P('head'), may hold values from -0.25 to 0.25
- w_down: bfloat16 [2, 512, 512], P('head'), may hold values from -0.25 to 0.25
- out_gain: float32 [2, 512], P('head'), may hold values from 0.1 to 1.9
- cotangent: bfloat16 [2, 4096, 512], P('head', 'tok'), may hold values from -6 to 6
Outputs:
- grad_queries: bfloat16 [2, 4096, 512], P('head', 'tok')
- grad_keys: bfloat16 [2, 4096, 512], P('head', 'tok')
- grad_values: bfloat16 [2, 4096, 512], P('head', 'tok')
- grad_gate: float32 [2, 512, 512], P('head', 'tok')
- grad_up: float32 [2, 512, 512], P('head', 'tok')
- grad_down: float32 [2, 512, 512], P('head', 'tok')
The draws below stay inside these ranges and needn't reach their ends.
All inputs are finite; a program needn't handle non-finite values.
Results may differ from the reference program's by a relative error of at most 0.03.
Values sent between devices are 32-bit elements; how exact they have to be, the bound alone decides.
A program may use at most 128 MiB of HBM per device.

```python
import math
import jax
import jax.numpy as jnp
from jax import lax

H = 2
DH = 512
NS_STEPS = 3
TOKENS = 4096


def level_of(own_key, extent, pieces, least, high):
    level, own = 1.0, jax.random.fold_in(own_key, 6)
    for position, shards_of in pieces:
        draws = jnp.exp(jax.random.uniform(jax.random.fold_in(own, position), (shards_of,), jnp.float32, least / len(pieces), high / len(pieces)))
        level = level * jnp.repeat(draws, extent[position] // shards_of).reshape([-1 if axis == position else 1 for axis in range(len(extent))])
    return level


def scatter_about(own_key, shape, deviation, bound, pieces=(), kind=jnp.bfloat16):
    drawn = jax.random.normal(own_key, shape, jnp.float32) * deviation
    if len(pieces) > 0:
        drawn = level_of(own_key, shape, pieces, -0.22, 0.18) * drawn
    return jnp.clip(drawn, min=-bound, max=bound).astype(kind)


def setup_inputs(seed: int = 0) -> dict:
    splits = jax.random.split(jax.random.key(seed), 10)
    return {
        "queries": scatter_about(splits[0], (H, TOKENS, DH), 1.0, 6.0, ((0, 2), (1, 16))),
        "key_rows": scatter_about(splits[1], (H, TOKENS, DH), 1.0, 6.0, ((0, 2), (1, 16))),
        "value_rows": scatter_about(splits[2], (H, TOKENS, DH), 1.0, 6.0, ((0, 2), (1, 16))),
        "step_rates": jnp.clip(jnp.exp(math.log(1.0) - 2.3025851 * jax.random.uniform(splits[3], (H, TOKENS), jnp.float32) ** level_of(splits[3], (H, TOKENS), ((0, 2), (1, 16)), -0.2, 0.2)), 0.1, 1.0),
        "w_gate": scatter_about(splits[4], (H, DH, DH), DH ** -0.5, 0.25, ((0, 2),)),
        "w_up": scatter_about(splits[5], (H, DH, DH), DH ** -0.5, 0.25, ((0, 2),)),
        "w_down": scatter_about(splits[6], (H, DH, DH), DH ** -0.5, 0.25, ((0, 2),)),
        "out_gain": jnp.clip(1.0 + 0.18 * jax.random.normal(splits[7], (H, DH), jnp.float32), 0.1, 1.9),
        "cotangent": scatter_about(splits[8], (H, TOKENS, DH), 1.0, 6.0, ((0, 2), (1, 16))),
    }


coef_first = 3.4445
coef_second = -4.775
coef_third = 2.0315
inner_step = 0.5

def contract_rows(first_op, second_op):
    return lax.dot_general(first_op, second_op, (((0,), (0,)), ((), ())), preferred_element_type=jnp.float32)

def contract_cols(first_op, second_op):
    return lax.dot_general(first_op, second_op, (((1,), (1,)), ((), ())), preferred_element_type=jnp.float32)

def silu_parts(pre_gate):
    sigma_gate = jax.nn.sigmoid(pre_gate)
    act_gate = pre_gate * sigma_gate
    slope_gate = sigma_gate * (1.0 + pre_gate * (1.0 - sigma_gate))
    return (act_gate, slope_gate, sigma_gate)

def orthogonalize(matrix):
    current = matrix / jnp.sqrt(jnp.sum(matrix * matrix) + 1e-06)
    for iteration in range(NS_STEPS):
        narrow = current.astype(jnp.bfloat16)
        gram_matrix = contract_cols(narrow, narrow)
        gram_low = gram_matrix.astype(jnp.bfloat16)
        poly_term = (coef_second * gram_matrix + coef_third * jnp.dot(gram_low, gram_low, preferred_element_type=jnp.float32)).astype(jnp.bfloat16)
        current = coef_first * current + jnp.dot(poly_term, narrow, preferred_element_type=jnp.float32)
    return current

def orthogonalize_all(grad_triple):
    mapped = jax.vmap(orthogonalize)
    return (mapped(grad_triple[0]), mapped(grad_triple[1]), mapped(grad_triple[2]))

def key_forward(w_gate, w_up, w_down, key_rows, value_rows, step_rates):
    key_gate = jnp.dot(key_rows, w_gate, preferred_element_type=jnp.float32)
    key_up = jnp.dot(key_rows, w_up, preferred_element_type=jnp.float32)
    act_gate, slope_gate, sigma_gate = silu_parts(key_gate)
    key_mixed = (act_gate * key_up).astype(jnp.bfloat16)
    target = (-step_rates[:, None] * value_rows).astype(jnp.bfloat16)
    key_mid = contract_cols(target, w_down)
    key_dgate = (key_mid * key_up * slope_gate).astype(jnp.bfloat16)
    key_dup = (key_mid * act_gate).astype(jnp.bfloat16)
    inner_grads = (contract_rows(key_rows, key_dgate), contract_rows(key_rows, key_dup), contract_rows(key_mixed, target))
    stored = (key_gate, key_up, act_gate, slope_gate, sigma_gate, key_mixed, target, key_mid, key_dgate, key_dup)
    return (inner_grads, stored)

def key_backward(w_gate, w_up, w_down, key_rows, step_rates, stored, back_a, back_b, back_c):
    key_gate, key_up, act_gate, slope_gate, sigma_gate, key_mixed, target, key_mid, key_dgate, key_dup = stored
    cot_a = back_a.astype(jnp.bfloat16)
    cot_b = back_b.astype(jnp.bfloat16)
    cot_c = back_c.astype(jnp.bfloat16)
    back_gate = jnp.dot(key_rows, cot_a, preferred_element_type=jnp.float32)
    back_up = jnp.dot(key_rows, cot_b, preferred_element_type=jnp.float32)
    back_mixed = contract_cols(target, cot_c)
    back_target = jnp.dot(key_mixed, cot_c, preferred_element_type=jnp.float32)
    curve_gate = sigma_gate * (1.0 - sigma_gate) * (2.0 + key_gate * (1.0 - 2.0 * sigma_gate))
    back_mid = (back_gate * key_up * slope_gate + back_up * act_gate).astype(jnp.bfloat16)
    gate_back = (back_gate * key_mid * key_up * curve_gate + back_up * key_mid * slope_gate + back_mixed * key_up * slope_gate).astype(jnp.bfloat16)
    up_back = (back_gate * key_mid * slope_gate + back_mixed * act_gate).astype(jnp.bfloat16)
    key_grad = contract_cols(key_dgate, cot_a) + contract_cols(key_dup, cot_b) + contract_cols(gate_back, w_gate) + contract_cols(up_back, w_up)
    value_sum = back_target + jnp.dot(back_mid, w_down, preferred_element_type=jnp.float32)
    value_grad = (-step_rates[:, None] * value_sum).astype(jnp.bfloat16)
    weight_terms = jnp.concatenate([contract_rows(key_rows, gate_back), contract_rows(key_rows, up_back), contract_rows(back_mid, target)], axis=1)
    return (key_grad.astype(jnp.bfloat16), value_grad, weight_terms)

def query_forward(new_gate, new_up, new_down, queries):
    query_gate = jnp.dot(queries, new_gate, preferred_element_type=jnp.float32)
    query_up = jnp.dot(queries, new_up, preferred_element_type=jnp.float32)
    act_gate, slope_gate, sigma_gate = silu_parts(query_gate)
    query_mixed = (act_gate * query_up).astype(jnp.bfloat16)
    output = jnp.dot(query_mixed, new_down, preferred_element_type=jnp.float32)
    return (output, (query_up, act_gate, slope_gate, query_mixed))

def query_backward(new_gate, new_up, new_down, queries, stored, grad_output):
    query_up, act_gate, slope_gate, query_mixed = stored
    query_mid = contract_cols(grad_output, new_down)
    query_dgate = (query_mid * query_up * slope_gate).astype(jnp.bfloat16)
    query_dup = (query_mid * act_gate).astype(jnp.bfloat16)
    query_grad = (contract_cols(query_dgate, new_gate) + contract_cols(query_dup, new_up)).astype(jnp.bfloat16)
    weight_terms = jnp.concatenate([contract_rows(queries, query_dgate), contract_rows(queries, query_dup), contract_rows(query_mixed, grad_output)], axis=1)
    return (query_grad, weight_terms)

def reference(queries, key_rows, value_rows, step_rates, w_gate, w_up, w_down, out_gain, cotangent):
    inner_grads, stored = jax.vmap(key_forward)(w_gate, w_up, w_down, key_rows, value_rows, step_rates)
    unitary, ns_back = jax.vjp(orthogonalize_all, inner_grads)
    new_gate = (w_gate - inner_step * unitary[0]).astype(jnp.bfloat16)
    new_up = (w_up - inner_step * unitary[1]).astype(jnp.bfloat16)
    new_down = (w_down - inner_step * unitary[2]).astype(jnp.bfloat16)
    output, query_stored = jax.vmap(query_forward)(new_gate, new_up, new_down, queries)
    full_width = H * DH
    squares = lax.optimization_barrier(jnp.sum(output * output, axis=(0, 2)))
    gain_wide = out_gain[:, None, :]
    aligned = lax.optimization_barrier(jnp.sum(cotangent * gain_wide * output, axis=(0, 2)))
    inverse_rms = lax.rsqrt(squares / full_width + 1e-05)
    grad_output = (gain_wide * cotangent * inverse_rms[None, :, None] - output * (aligned * inverse_rms * inverse_rms * inverse_rms / full_width)[None, :, None]).astype(jnp.bfloat16)
    query_grad, query_terms = jax.vmap(query_backward)(new_gate, new_up, new_down, queries, query_stored, grad_output)
    outer_back = (-inner_step * query_terms[:, :, :DH], -inner_step * query_terms[:, :, DH:2 * DH], -inner_step * query_terms[:, :, 2 * DH:])
    back_triple = ns_back(outer_back)[0]
    key_grad, value_grad, key_terms = jax.vmap(key_backward)(w_gate, w_up, w_down, key_rows, step_rates, stored, back_triple[0], back_triple[1], back_triple[2])
    weight_total = query_terms + key_terms
    return (query_grad, key_grad, value_grad, weight_total[:, :, :DH], weight_total[:, :, DH:2 * DH], weight_total[:, :, 2 * DH:])
```

```python
import jax
import jax.numpy as jnp
from jax import lax
from jax.experimental import pallas as pl
from jax.experimental.pallas import tpu as pltpu
from jax.sharding import PartitionSpec as P

NS_STEPS = 3


coef_first = 3.4445
coef_second = -4.775
coef_third = 2.0315
inner_step = 0.5


def contract_rows(first_op, second_op):
    return lax.dot_general(
        first_op, second_op, (((0,), (0,)), ((), ())), preferred_element_type=jnp.float32
    )


def contract_cols(first_op, second_op):
    return lax.dot_general(
        first_op, second_op, (((1,), (1,)), ((), ())), preferred_element_type=jnp.float32
    )


def silu_parts(pre_gate):
    sigma_gate = jax.nn.sigmoid(pre_gate)
    act_gate = pre_gate * sigma_gate
    slope_gate = sigma_gate * (1.0 + pre_gate * (1.0 - sigma_gate))
    return (act_gate, slope_gate, sigma_gate)


def orthogonalize(matrix):
    current = matrix / jnp.sqrt(jnp.sum(matrix * matrix) + 1e-06)
    for iteration in range(NS_STEPS):
        narrow = current.astype(jnp.bfloat16)
        gram_matrix = contract_cols(narrow, narrow)
        gram_low = gram_matrix.astype(jnp.bfloat16)
        poly_term = (
            coef_second * gram_matrix
            + coef_third * jnp.dot(gram_low, gram_low, preferred_element_type=jnp.float32)
        ).astype(jnp.bfloat16)
        current = coef_first * current + jnp.dot(
            poly_term, narrow, preferred_element_type=jnp.float32
        )
    return current


def orthogonalize_all(grad_triple):
    mapped = jax.vmap(orthogonalize)
    return (mapped(grad_triple[0]), mapped(grad_triple[1]), mapped(grad_triple[2]))


def key_forward(w_gate, w_up, w_down, key_rows, value_rows, step_rates):
    key_gate = jnp.dot(key_rows, w_gate, preferred_element_type=jnp.float32)
    key_up = jnp.dot(key_rows, w_up, preferred_element_type=jnp.float32)
    act_gate, slope_gate, sigma_gate = silu_parts(key_gate)
    key_mixed = (act_gate * key_up).astype(jnp.bfloat16)
    target = (-step_rates[:, None] * value_rows).astype(jnp.bfloat16)
    key_mid = contract_cols(target, w_down)
    key_dgate = (key_mid * key_up * slope_gate).astype(jnp.bfloat16)
    key_dup = (key_mid * act_gate).astype(jnp.bfloat16)
    inner_grads = (
        contract_rows(key_rows, key_dgate),
        contract_rows(key_rows, key_dup),
        contract_rows(key_mixed, target),
    )
    stored = (
        key_gate,
        key_up,
        act_gate,
        slope_gate,
        sigma_gate,
        key_mixed,
        target,
        key_mid,
        key_dgate,
        key_dup,
    )
    return (inner_grads, stored)


def key_backward(w_gate, w_up, w_down, key_rows, step_rates, stored, back_a, back_b, back_c):
    (
        key_gate,
        key_up,
        act_gate,
        slope_gate,
        sigma_gate,
        key_mixed,
        target,
        key_mid,
        key_dgate,
        key_dup,
    ) = stored
    cot_a = back_a.astype(jnp.bfloat16)
    cot_b = back_b.astype(jnp.bfloat16)
    cot_c = back_c.astype(jnp.bfloat16)
    back_gate = jnp.dot(key_rows, cot_a, preferred_element_type=jnp.float32)
    back_up = jnp.dot(key_rows, cot_b, preferred_element_type=jnp.float32)
    back_mixed = contract_cols(target, cot_c)
    back_target = jnp.dot(key_mixed, cot_c, preferred_element_type=jnp.float32)
    curve_gate = sigma_gate * (1.0 - sigma_gate) * (2.0 + key_gate * (1.0 - 2.0 * sigma_gate))
    back_mid = (back_gate * key_up * slope_gate + back_up * act_gate).astype(jnp.bfloat16)
    gate_back = (
        back_gate * key_mid * key_up * curve_gate
        + back_up * key_mid * slope_gate
        + back_mixed * key_up * slope_gate
    ).astype(jnp.bfloat16)
    up_back = (back_gate * key_mid * slope_gate + back_mixed * act_gate).astype(jnp.bfloat16)
    key_grad = (
        contract_cols(key_dgate, cot_a)
        + contract_cols(key_dup, cot_b)
        + contract_cols(gate_back, w_gate)
        + contract_cols(up_back, w_up)
    )
    value_sum = back_target + jnp.dot(back_mid, w_down, preferred_element_type=jnp.float32)
    value_grad = (-step_rates[:, None] * value_sum).astype(jnp.bfloat16)
    weight_terms = (
            contract_rows(key_rows, gate_back),
            contract_rows(key_rows, up_back),
            contract_rows(back_mid, target),
        )
    return (key_grad.astype(jnp.bfloat16), value_grad, weight_terms)


def query_forward(new_gate, new_up, new_down, queries):
    query_gate = jnp.dot(queries, new_gate, preferred_element_type=jnp.float32)
    query_up = jnp.dot(queries, new_up, preferred_element_type=jnp.float32)
    act_gate, slope_gate, sigma_gate = silu_parts(query_gate)
    query_mixed = (act_gate * query_up).astype(jnp.bfloat16)
    output = jnp.dot(query_mixed, new_down, preferred_element_type=jnp.float32)
    return (output, (query_up, act_gate, slope_gate, query_mixed))


def query_backward(new_gate, new_up, new_down, queries, stored, grad_output):
    query_up, act_gate, slope_gate, query_mixed = stored
    query_mid = contract_cols(grad_output, new_down)
    query_dgate = (query_mid * query_up * slope_gate).astype(jnp.bfloat16)
    query_dup = (query_mid * act_gate).astype(jnp.bfloat16)
    query_grad = (contract_cols(query_dgate, new_gate) + contract_cols(query_dup, new_up)).astype(
        jnp.bfloat16
    )
    weight_terms = (
            contract_rows(queries, query_dgate),
            contract_rows(queries, query_dup),
            contract_rows(query_mixed, grad_output),
        )
    return (query_grad, weight_terms)


def bit_orders(bits):
    plain = tuple(range(bits))
    if bits < 3:
        return (plain, plain[::-1])
    swapped = (1, 0) + plain[2:]
    return (plain, swapped, (2, 0, 1) + plain[3:], plain, swapped, (2, 1, 0) + plain[3:])


def sum_over_tok(arrays, devices, call_id, whole):
    bits = devices.bit_length() - 1
    rows, columns = arrays[0].shape
    block = rows // devices
    width = 128
    count = len(arrays)
    orders = bit_orders(bits)
    streams = [
        (array, pl.ds(start, width))
        for array in range(count)
        for start in range(0, columns, width)
    ]
    split = (2,) * bits + (block,)

    def kernel(*refs):
        given = refs[:count]
        shares = refs[count : 2 * count]
        position = 2 * count
        wholes = refs[position : position + count] if whole else ()
        position += len(wholes)
        partial = refs[position : position + count]
        landing = refs[position + count : position + count + bits]
        sems = refs[position + count + bits :]
        me = lax.axis_index("tok")
        mine = [lax.rem(lax.div(me, 1 << bit), 2) for bit in range(bits)]
        partner = [me + (1 - 2 * mine[bit]) * (1 << bit) for bit in range(bits)]

        barrier = pltpu.get_barrier_semaphore()
        for bit in range(bits):
            pl.semaphore_signal(
                barrier,
                inc=1,
                device_id={"tok": partner[bit]},
                device_id_type=pl.DeviceIdType.MESH,
            )
        pl.semaphore_wait(barrier, bits)

        def pick(fixed, lanes):
            leading = tuple(fixed.get(bit, slice(None)) for bit in reversed(range(bits)))
            return leading + (slice(None), lanes)

        sent = []

        def send(source, target, stream, stage, phase, bit):
            copy = pltpu.make_async_remote_copy(
                src_ref=source,
                dst_ref=target,
                send_sem=sems[2 * phase].at[stream, stage],
                recv_sem=sems[2 * phase + 1].at[stream, stage],
                device_id={"tok": partner[bit]},
                device_id_type=pl.DeviceIdType.MESH,
            )
            copy.start()
            sent.append(copy)
            return copy

        def halve(stream, stage):
            array, lanes = streams[stream]
            order = orders[stream % len(orders)]
            fixed = {bit: mine[bit] for bit in order[:stage]}
            bit = order[stage]
            fixed[bit] = 1 - mine[bit]
            held = given[array] if stage == 0 else partial[array]
            return send(
                held.at[pick(fixed, lanes)], landing[stage].at[stream], stream, stage, 0, bit
            )

        def double(stream, stage):
            array, lanes = streams[stream]
            order = orders[stream % len(orders)]
            region = wholes[array].at[pick({bit: mine[bit] for bit in order[: stage + 1]}, lanes)]
            return send(region, region, stream, stage, 1, order[stage])

        flying = [halve(stream, 0) for stream in range(len(streams))]
        for stage in range(bits):
            for stream, (array, lanes) in enumerate(streams):
                order = orders[stream % len(orders)]
                flying[stream].wait_recv()
                kept = pick({bit: mine[bit] for bit in order[: stage + 1]}, lanes)
                held = given[array] if stage == 0 else partial[array]
                total = held[kept] + landing[stage][stream]
                if stage < bits - 1:
                    partial[array][kept] = total
                    flying[stream] = halve(stream, stage + 1)
                else:
                    shares[array][:, lanes] = total
                    if whole:
                        wholes[array][kept] = total
                        flying[stream] = double(stream, stage)
        if whole:
            for stage in reversed(range(bits)):
                for stream in range(len(streams)):
                    flying[stream].wait_recv()
                    if stage > 0:
                        flying[stream] = double(stream, stage - 1)
        for copy in sent:
            copy.wait_send()

    phases = 2 if whole else 1
    outs = [jax.ShapeDtypeStruct((block, columns), jnp.float32)] * count
    if whole:
        outs += [jax.ShapeDtypeStruct(split + (columns,), jnp.float32)] * count
    vmem = pl.BlockSpec(memory_space=pltpu.VMEM)
    results = pl.pallas_call(
        kernel,
        out_shape=outs,
        in_specs=[vmem] * count,
        out_specs=[vmem] * len(outs),
        scratch_shapes=[pltpu.VMEM(split + (columns,), jnp.float32)] * count
        + [
            pltpu.VMEM((len(streams),) + (2,) * (bits - 1 - stage) + (block, width), jnp.float32)
            for stage in range(bits)
        ]
        + [pltpu.SemaphoreType.DMA((len(streams), bits))] * (2 * phases),
        compiler_params=pltpu.CompilerParams(collective_id=call_id, has_side_effects=True),
        name="sum_whole" if whole else "sum_share",
    )(*[array.reshape(split + (columns,)) for array in arrays])
    shares = results[:count]
    return shares, [array.reshape(rows, columns) for array in results[count:]]


def local(queries, key_rows, value_rows, step_rates, w_gate, w_up, w_down, out_gain, cotangent):
    head_size = w_gate.shape[2]
    local_grads, stored = jax.vmap(key_forward)(
        w_gate, w_up, w_down, key_rows, value_rows, step_rates
    )
    devices = lax.axis_size("tok")
    inner_wholes = sum_over_tok([grad[0] for grad in local_grads], devices, 0, True)[1]
    inner_grads = tuple(grad[None] for grad in inner_wholes)
    unitary, ns_back = jax.vjp(orthogonalize_all, inner_grads)
    new_gate = (w_gate - inner_step * unitary[0]).astype(jnp.bfloat16)
    new_up = (w_up - inner_step * unitary[1]).astype(jnp.bfloat16)
    new_down = (w_down - inner_step * unitary[2]).astype(jnp.bfloat16)
    output, query_stored = jax.vmap(query_forward)(new_gate, new_up, new_down, queries)
    full_width = queries.shape[0] * lax.axis_size("head") * head_size
    squares_local = jnp.sum(output * output, axis=(0, 2))
    gain_wide = out_gain[:, None, :]
    squares, aligned = lax.psum(
        (squares_local, jnp.sum(cotangent * gain_wide * output, axis=(0, 2))), "head"
    )
    inverse_rms = lax.rsqrt(squares / full_width + 1e-05)
    grad_output = (
        gain_wide * cotangent * inverse_rms[None, :, None]
        - output * (aligned * inverse_rms * inverse_rms * inverse_rms / full_width)[None, :, None]
    ).astype(jnp.bfloat16)
    query_grad, query_terms = jax.vmap(query_backward)(
        new_gate, new_up, new_down, queries, query_stored, grad_output
    )
    query_shares, query_wholes = sum_over_tok([term[0] for term in query_terms], devices, 1, True)
    outer_back = tuple(-inner_step * term[None] for term in query_wholes)
    back_triple = ns_back(outer_back)[0]
    key_grad, value_grad, key_terms = jax.vmap(key_backward)(
        w_gate,
        w_up,
        w_down,
        key_rows,
        step_rates,
        stored,
        back_triple[0],
        back_triple[1],
        back_triple[2],
    )
    key_shares, _ = sum_over_tok([term[0] for term in key_terms], devices, 2, False)
    return (query_grad, key_grad, value_grad) + tuple(
        (query_share + key_share)[None] for query_share, key_share in zip(query_shares, key_shares)
    )


def solution(mesh):
    in_specs = (
        P("head", "tok", None),
        P("head", "tok", None),
        P("head", "tok", None),
        P("head", "tok"),
        P("head", None, None),
        P("head", None, None),
        P("head", None, None),
        P("head", None),
        P("head", "tok", None),
    )
    out_specs = (
        P("head", "tok", None),
        P("head", "tok", None),
        P("head", "tok", None),
        P("head", "tok", None),
        P("head", "tok", None),
        P("head", "tok", None),
    )
    return jax.shard_map(local, mesh=mesh, in_specs=in_specs, out_specs=out_specs, check_vma=False)
```

```python
import jax
import jax.numpy as jnp
from jax import lax
from jax.experimental import pallas as pl
from jax.experimental.pallas import tpu as pltpu
from jax.sharding import PartitionSpec as P

NS_STEPS = 3
WAVE = 3
AHEAD = 1


coef_first = 3.4445
coef_second = -4.775
coef_third = 2.0315
inner_step = 0.5


def silu_parts(pre_gate):
    sigma_gate = jax.nn.sigmoid(pre_gate)
    act_gate = pre_gate * sigma_gate
    slope_gate = sigma_gate * (1.0 + pre_gate * (1.0 - sigma_gate))
    return (act_gate, slope_gate, sigma_gate)


def mxu(first_op, second_op, first_dim, second_dim):
    return lax.dot_general(
        first_op,
        second_op,
        (((first_dim,), (second_dim,)), ((), ())),
        preferred_element_type=jnp.float32,
    )


def unitary_forward(inner_grads, weights):
    size = weights[0].shape[0]
    count = len(weights)

    def kernel(*refs):
        matrices, olds = refs[:count], refs[count : 2 * count]
        new_ref, narrow_ref, gram_ref, poly_ref, current = refs[2 * count :]
        for which in range(count):

            @pl.when(pl.program_id(0) == which)
            def _(which=which):
                matrix = matrices[which][...]
                current[...] = matrix / jnp.sqrt(jnp.sum(matrix * matrix) + 1e-06)

        def step(iteration, carry):
            narrow = current[...].astype(jnp.bfloat16)
            narrow_ref[0, iteration] = narrow
            gram = mxu(narrow, narrow, 1, 1)
            gram_low = gram.astype(jnp.bfloat16)
            gram_ref[0, iteration] = gram_low
            poly = (coef_second * gram + coef_third * mxu(gram_low, gram_low, 1, 0)).astype(
                jnp.bfloat16
            )
            poly_ref[0, iteration] = poly
            current[...] = coef_first * current[...] + mxu(poly, narrow, 1, 0)
            return carry

        lax.fori_loop(0, NS_STEPS, step, 0)
        for which in range(count):

            @pl.when(pl.program_id(0) == which)
            def _(which=which):
                old = olds[which][...].astype(jnp.float32)
                new_ref[0] = (old - inner_step * current[...]).astype(jnp.bfloat16)

    vmem = pl.BlockSpec(memory_space=pltpu.VMEM)
    saved = jax.ShapeDtypeStruct((count, NS_STEPS, size, size), jnp.bfloat16)
    saved_spec = pl.BlockSpec((1, NS_STEPS, size, size), lambda i: (i, 0, 0, 0))
    return pl.pallas_call(
        kernel,
        grid=(count,),
        out_shape=[jax.ShapeDtypeStruct((count, size, size), jnp.bfloat16), saved, saved, saved],
        in_specs=[vmem] * (2 * count),
        out_specs=[pl.BlockSpec((1, size, size), lambda i: (i, 0, 0))] + [saved_spec] * 3,
        scratch_shapes=[pltpu.VMEM((size, size), jnp.float32)],
        name="unitary_forward",
    )(*inner_grads, *weights)


def unitary_backward(inner_grads, outer_grads, saved):
    size = inner_grads[0].shape[0]
    count = len(inner_grads)

    def kernel(*refs):
        matrices, outers = refs[:count], refs[count : 2 * count]
        narrow_ref, gram_ref, poly_ref, cot_ref, grad = refs[2 * count :]
        for which in range(count):

            @pl.when(pl.program_id(0) == which)
            def _(which=which):
                grad[...] = -inner_step * outers[which][...]

        def step(back_iteration, carry):
            iteration = NS_STEPS - 1 - back_iteration
            narrow = narrow_ref[0, iteration]
            gram_low = gram_ref[0, iteration]
            grad_low = grad[...].astype(jnp.bfloat16)
            poly_grad = mxu(grad_low, narrow, 1, 1).astype(jnp.bfloat16).astype(jnp.float32)
            pair = poly_grad + poly_grad.T
            product = mxu(pair.astype(jnp.bfloat16), gram_low, 1, 0)
            gram_grad = coef_second * pair + coef_third * (product + product.T)
            narrow_grad = mxu(poly_ref[0, iteration], grad_low, 0, 0) + mxu(
                gram_grad.astype(jnp.bfloat16), narrow, 1, 0
            )
            grad[...] = coef_first * grad[...] + narrow_grad.astype(jnp.bfloat16).astype(
                jnp.float32
            )
            return carry

        lax.fori_loop(0, NS_STEPS, step, 0)
        for which in range(count):

            @pl.when(pl.program_id(0) == which)
            def _(which=which):
                matrix = matrices[which][...]
                inverse = lax.rsqrt(jnp.sum(matrix * matrix) + 1e-06)
                along = jnp.sum(matrix * grad[...]) * inverse * inverse * inverse
                cot_ref[0] = (grad[...] * inverse - matrix * along).astype(jnp.bfloat16)

    vmem = pl.BlockSpec(memory_space=pltpu.VMEM)
    saved_spec = pl.BlockSpec((1, NS_STEPS, size, size), lambda i: (i, 0, 0, 0))
    return pl.pallas_call(
        kernel,
        grid=(count,),
        out_shape=jax.ShapeDtypeStruct((count, size, size), jnp.bfloat16),
        in_specs=[vmem] * (2 * count) + [saved_spec] * 3,
        out_specs=pl.BlockSpec((1, size, size), lambda i: (i, 0, 0)),
        scratch_shapes=[pltpu.VMEM((size, size), jnp.float32)],
        name="unitary_backward",
    )(*inner_grads, *outer_grads, *saved)


def on_core(kernel, name, outs, *operands):
    vmem = pl.BlockSpec(memory_space=pltpu.VMEM)
    return pl.pallas_call(
        kernel,
        out_shape=[jax.ShapeDtypeStruct(shape, kind) for shape, kind in outs],
        in_specs=[vmem] * len(operands),
        out_specs=[vmem] * len(outs),
        name=name,
    )(*operands)


def key_forward(w_gate, w_up, w_down, key_rows, value_rows, step_rates):
    def kernel(gate_w, up_w, down_w, keys, values, rates, a, b, c, gate, up, mid, mixed, target, dgate, dup):
        rows = keys[...]
        key_gate = mxu(rows, gate_w[...], 1, 0)
        key_up = mxu(rows, up_w[...], 1, 0)
        aim = (-rates[...] * values[...].astype(jnp.float32)).astype(jnp.bfloat16)
        key_mid = mxu(aim, down_w[...], 1, 1)
        act_gate, slope_gate, _ = silu_parts(key_gate)
        gate[...] = key_gate
        up[...] = key_up
        mid[...] = key_mid
        target[...] = aim
        mixed[...] = (act_gate * key_up).astype(jnp.bfloat16)
        dgate[...] = (key_mid * key_up * slope_gate).astype(jnp.bfloat16)
        dup[...] = (key_mid * act_gate).astype(jnp.bfloat16)
        a[...] = mxu(rows, dgate[...], 0, 0)
        b[...] = mxu(rows, dup[...], 0, 0)
        c[...] = mxu(mixed[...], target[...], 0, 0)

    square = (w_gate.shape, jnp.float32)
    wide, narrow = (key_rows.shape, jnp.float32), (key_rows.shape, jnp.bfloat16)
    results = on_core(
        kernel,
        "key_forward",
        [square] * 3 + [wide] * 3 + [narrow] * 4,
        w_gate,
        w_up,
        w_down,
        key_rows,
        value_rows,
        step_rates[:, None],
    )
    return results[:3], results[3:]


def key_backward(w_gate, w_up, w_down, key_rows, step_rates, stored, cots):
    def kernel(
        gate_w, up_w, down_w, keys, rates, gate, up, mid, mixed, target, dgate, dup, cots,
        key_grad, value_grad, a, b, c, mid_low, gate_low, up_low,
    ):
        rows = keys[...]
        back_gate = mxu(rows, cots[0], 1, 0)
        back_up = mxu(rows, cots[1], 1, 0)
        back_mixed = mxu(target[...], cots[2], 1, 1)
        key_gate, key_up, key_mid = gate[...], up[...], mid[...]
        act_gate, slope_gate, sigma_gate = silu_parts(key_gate)
        curve_gate = (
            sigma_gate * (1.0 - sigma_gate) * (2.0 + key_gate * (1.0 - 2.0 * sigma_gate))
        )
        mid_low[...] = (back_gate * key_up * slope_gate + back_up * act_gate).astype(jnp.bfloat16)
        gate_low[...] = (
            back_gate * key_mid * key_up * curve_gate
            + back_up * key_mid * slope_gate
            + back_mixed * key_up * slope_gate
        ).astype(jnp.bfloat16)
        up_low[...] = (back_gate * key_mid * slope_gate + back_mixed * act_gate).astype(
            jnp.bfloat16
        )
        a[...] = mxu(rows, gate_low[...], 0, 0)
        b[...] = mxu(rows, up_low[...], 0, 0)
        c[...] = mxu(mid_low[...], target[...], 0, 0)
        key_grad[...] = (
            mxu(dgate[...], cots[0], 1, 1)
            + mxu(dup[...], cots[1], 1, 1)
            + mxu(gate_low[...], gate_w[...], 1, 1)
            + mxu(up_low[...], up_w[...], 1, 1)
        ).astype(jnp.bfloat16)
        value_sum = mxu(mixed[...], cots[2], 1, 0) + mxu(mid_low[...], down_w[...], 1, 0)
        value_grad[...] = (-rates[...] * value_sum).astype(jnp.bfloat16)

    square = (w_gate.shape, jnp.float32)
    narrow = (key_rows.shape, jnp.bfloat16)
    results = on_core(
        kernel,
        "key_backward",
        [narrow] * 2 + [square] * 3 + [narrow] * 3,
        w_gate,
        w_up,
        w_down,
        key_rows,
        step_rates[:, None],
        *stored,
        cots,
    )
    return results[0], results[1], results[2:5]


def query_forward(news, queries, out_gain, cotangent):
    def kernel(news, rows, gain, cot, sums, gate, up, mixed, output):
        query_gate = mxu(rows[...], news[0], 1, 0)
        query_up = mxu(rows[...], news[1], 1, 0)
        gate[...] = query_gate
        up[...] = query_up
        act_gate, _, _ = silu_parts(query_gate)
        mixed[...] = (act_gate * query_up).astype(jnp.bfloat16)
        out = mxu(mixed[...], news[2], 1, 0)
        output[...] = out
        squares = jnp.sum(out * out, axis=1, keepdims=True)
        aligned = jnp.sum(cot[...].astype(jnp.float32) * gain[...] * out, axis=1, keepdims=True)
        lane = lax.broadcasted_iota(jnp.int32, sums.shape, 1)
        sums[...] = jnp.where(lane < sums.shape[1] // 2, squares, aligned)

    wide, narrow = (queries.shape, jnp.float32), (queries.shape, jnp.bfloat16)
    results = on_core(
        kernel,
        "query_forward",
        [((queries.shape[0], 128), jnp.float32), wide, wide, narrow, wide],
        news,
        queries,
        out_gain,
        cotangent,
    )
    return results[0], results[1:]


def query_backward(news, queries, out_gain, cotangent, sums, stored, full_width):
    def kernel(news, rows, gain, cot, sums, gate, up, mixed, output, query_grad, a, b, c, grad, dgate, dup):
        squares = sums[:, :1]
        aligned = sums[:, sums.shape[1] // 2 : sums.shape[1] // 2 + 1]
        inverse_rms = lax.rsqrt(squares / full_width + 1e-05)
        pull = aligned * inverse_rms * inverse_rms * inverse_rms / full_width
        grad[...] = (
            gain[...] * cot[...].astype(jnp.float32) * inverse_rms - output[...] * pull
        ).astype(jnp.bfloat16)
        query_mid = mxu(grad[...], news[2], 1, 1)
        act_gate, slope_gate, _ = silu_parts(gate[...])
        dgate[...] = (query_mid * up[...] * slope_gate).astype(jnp.bfloat16)
        dup[...] = (query_mid * act_gate).astype(jnp.bfloat16)
        a[...] = mxu(rows[...], dgate[...], 0, 0)
        b[...] = mxu(rows[...], dup[...], 0, 0)
        c[...] = mxu(mixed[...], grad[...], 0, 0)
        query_grad[...] = (
            mxu(dgate[...], news[0], 1, 1) + mxu(dup[...], news[1], 1, 1)
        ).astype(jnp.bfloat16)

    square = (news.shape[1:], jnp.float32)
    narrow = (queries.shape, jnp.bfloat16)
    results = on_core(
        kernel,
        "query_backward",
        [narrow] + [square] * 3 + [narrow] * 3,
        news,
        queries,
        out_gain,
        cotangent,
        sums,
        *stored,
    )
    return results[0], results[1:4]


def bit_orders(bits):
    plain = tuple(range(bits))
    if bits < 3:
        return (plain, plain[::-1])
    swapped = (1, 0) + plain[2:]
    return (plain, swapped, (2, 0, 1) + plain[3:], plain, swapped, (2, 1, 0) + plain[3:])


def sum_over_tok(arrays, devices, call_id, whole):
    bits = devices.bit_length() - 1
    rows, columns = arrays[0].shape
    block = rows // devices
    width = 128
    count = len(arrays)
    orders = bit_orders(bits)
    streams = [
        (array, pl.ds(start, width))
        for array in range(count)
        for start in range(0, columns, width)
    ]
    split = (2,) * bits + (block,)

    def kernel(*refs):
        given = refs[:count]
        shares = refs[count : 2 * count]
        position = 2 * count
        wholes = refs[position : position + count] if whole else ()
        position += len(wholes)
        partial = refs[position : position + count]
        landing = refs[position + count : position + count + bits]
        sems = refs[position + count + bits :]
        me = lax.axis_index("tok")
        mine = [lax.rem(lax.div(me, 1 << bit), 2) for bit in range(bits)]
        partner = [me + (1 - 2 * mine[bit]) * (1 << bit) for bit in range(bits)]

        barrier = pltpu.get_barrier_semaphore()
        for bit in range(bits):
            pl.semaphore_signal(
                barrier,
                inc=1,
                device_id={"tok": partner[bit]},
                device_id_type=pl.DeviceIdType.MESH,
            )
        pl.semaphore_wait(barrier, bits)

        def pick(fixed, lanes):
            leading = tuple(fixed.get(bit, slice(None)) for bit in reversed(range(bits)))
            return leading + (slice(None), lanes)

        sent = []

        def send(source, target, stream, stage, phase, bit):
            copy = pltpu.make_async_remote_copy(
                src_ref=source,
                dst_ref=target,
                send_sem=sems[2 * phase].at[stream, stage],
                recv_sem=sems[2 * phase + 1].at[stream, stage],
                device_id={"tok": partner[bit]},
                device_id_type=pl.DeviceIdType.MESH,
            )
            copy.start()
            sent.append(copy)
            return copy

        def halve(stream, stage):
            array, lanes = streams[stream]
            order = orders[stream % len(orders)]
            fixed = {bit: mine[bit] for bit in order[:stage]}
            bit = order[stage]
            fixed[bit] = 1 - mine[bit]
            held = given[array] if stage == 0 else partial[array]
            return send(
                held.at[pick(fixed, lanes)], landing[stage].at[stream], stream, stage, 0, bit
            )

        def double(stream, stage):
            array, lanes = streams[stream]
            order = orders[stream % len(orders)]
            region = wholes[array].at[pick({bit: mine[bit] for bit in order[: stage + 1]}, lanes)]
            return send(region, region, stream, stage, 1, order[stage])

        flying = {}

        def advance(stream, step):
            array, lanes = streams[stream]
            order = orders[stream % len(orders)]
            if step > 0:
                flying[stream].wait_recv()
            if 0 < step <= bits:
                stage = step - 1
                kept = pick({bit: mine[bit] for bit in order[:step]}, lanes)
                held = given[array] if stage == 0 else partial[array]
                total = held[kept] + landing[stage][stream]
                if step < bits:
                    partial[array][kept] = total
                else:
                    shares[array][:, lanes] = total
                    if whole:
                        wholes[array][kept] = total
            if step < bits:
                flying[stream] = halve(stream, step)
            elif step < steps:
                flying[stream] = double(stream, 2 * bits - 1 - step)

        steps = 2 * bits if whole else bits
        waves = [range(first, min(first + WAVE, len(streams))) for first in range(0, len(streams), WAVE)]
        begins = [max(0, wave - AHEAD) for wave in range(len(waves))]
        for tick in range(begins[-1] + steps + 1):
            for begin, wave in zip(begins, waves):
                if 0 <= tick - begin <= steps:
                    for stream in wave:
                        advance(stream, tick - begin)
        for copy in sent:
            copy.wait_send()

    phases = 2 if whole else 1
    outs = [jax.ShapeDtypeStruct((block, columns), jnp.float32)] * count
    if whole:
        outs += [jax.ShapeDtypeStruct(split + (columns,), jnp.float32)] * count
    vmem = pl.BlockSpec(memory_space=pltpu.VMEM)
    results = pl.pallas_call(
        kernel,
        out_shape=outs,
        in_specs=[vmem] * count,
        out_specs=[vmem] * len(outs),
        scratch_shapes=[pltpu.VMEM(split + (columns,), jnp.float32)] * count
        + [
            pltpu.VMEM((len(streams),) + (2,) * (bits - 1 - stage) + (block, width), jnp.float32)
            for stage in range(bits)
        ]
        + [pltpu.SemaphoreType.DMA((len(streams), bits))] * (2 * phases),
        compiler_params=pltpu.CompilerParams(collective_id=call_id, has_side_effects=True),
        name="sum_whole" if whole else "sum_share",
    )(*[array.reshape(split + (columns,)) for array in arrays])
    shares = results[:count]
    return shares, [array.reshape(rows, columns) for array in results[count:]]


def local(queries, key_rows, value_rows, step_rates, w_gate, w_up, w_down, out_gain, cotangent):
    heads_here, _, head_size = queries.shape
    assert heads_here == 1
    queries, key_rows, value_rows, step_rates, w_gate, w_up, w_down, cotangent = (
        array[0]
        for array in (
            queries, key_rows, value_rows, step_rates, w_gate, w_up, w_down, cotangent,
        )
    )
    devices = lax.axis_size("tok")
    full_width = lax.axis_size("head") * head_size
    local_grads, stored = key_forward(w_gate, w_up, w_down, key_rows, value_rows, step_rates)
    inner_grads = sum_over_tok(local_grads, devices, 0, True)[1]
    news, *saved = unitary_forward(inner_grads, (w_gate, w_up, w_down))
    sums, query_stored = query_forward(news, queries, out_gain, cotangent)
    sums = lax.psum(sums, "head")
    query_grad, query_terms = query_backward(
        news, queries, out_gain, cotangent, sums, query_stored, full_width
    )
    query_shares, outer_grads = sum_over_tok(query_terms, devices, 1, True)
    cots = unitary_backward(inner_grads, outer_grads, saved)
    key_grad, value_grad, key_terms = key_backward(
        w_gate, w_up, w_down, key_rows, step_rates, stored, cots
    )
    key_shares, _ = sum_over_tok(key_terms, devices, 2, False)
    return (query_grad[None], key_grad[None], value_grad[None]) + tuple(
        (query_share + key_share)[None] for query_share, key_share in zip(query_shares, key_shares)
    )


def solution(mesh):
    in_specs = (
        P("head", "tok", None),
        P("head", "tok", None),
        P("head", "tok", None),
        P("head", "tok"),
        P("head", None, None),
        P("head", None, None),
        P("head", None, None),
        P("head", None),
        P("head", "tok", None),
    )
    out_specs = (
        P("head", "tok", None),
        P("head", "tok", None),
        P("head", "tok", None),
        P("head", "tok", None),
        P("head", "tok", None),
        P("head", "tok", None),
    )
    return jax.shard_map(local, mesh=mesh, in_specs=in_specs, out_specs=out_specs, check_vma=False)
```

```python
import jax
import jax.numpy as jnp
from jax import lax
from jax.experimental import pallas as pl
from jax.experimental.pallas import tpu as pltpu
from jax.sharding import PartitionSpec as P

NS_STEPS = 3
WAVE = 12
AHEAD = 0


coef_first = 3.4445
coef_second = -4.775
coef_third = 2.0315
inner_step = 0.5


def silu_parts(pre_gate):
    sigma_gate = jax.nn.sigmoid(pre_gate)
    act_gate = pre_gate * sigma_gate
    slope_gate = sigma_gate * (1.0 + pre_gate * (1.0 - sigma_gate))
    return (act_gate, slope_gate, sigma_gate)


def mxu(first_op, second_op, first_dim, second_dim):
    return lax.dot_general(
        first_op,
        second_op,
        (((first_dim,), (second_dim,)), ((), ())),
        preferred_element_type=jnp.float32,
    )


def unitary_forward(inner_grads, weights):
    size = weights[0].shape[0]
    count = len(weights)

    def kernel(*refs):
        matrices, olds = refs[:count], refs[count : 2 * count]
        new_ref, narrow_ref, gram_ref, poly_ref, current = refs[2 * count :]
        for which in range(count):

            @pl.when(pl.program_id(0) == which)
            def _(which=which):
                matrix = matrices[which][...]
                current[...] = matrix / jnp.sqrt(jnp.sum(matrix * matrix) + 1e-06)

        def step(iteration, carry):
            narrow = current[...].astype(jnp.bfloat16)
            narrow_ref[0, iteration] = narrow
            gram = mxu(narrow, narrow, 1, 1)
            gram_low = gram.astype(jnp.bfloat16)
            gram_ref[0, iteration] = gram_low
            poly = (coef_second * gram + coef_third * mxu(gram_low, gram_low, 1, 0)).astype(
                jnp.bfloat16
            )
            poly_ref[0, iteration] = poly
            current[...] = coef_first * current[...] + mxu(poly, narrow, 1, 0)
            return carry

        lax.fori_loop(0, NS_STEPS, step, 0)
        for which in range(count):

            @pl.when(pl.program_id(0) == which)
            def _(which=which):
                old = olds[which][...].astype(jnp.float32)
                new_ref[0] = (old - inner_step * current[...]).astype(jnp.bfloat16)

    vmem = pl.BlockSpec(memory_space=pltpu.VMEM)
    saved = jax.ShapeDtypeStruct((count, NS_STEPS, size, size), jnp.bfloat16)
    saved_spec = pl.BlockSpec((1, NS_STEPS, size, size), lambda i: (i, 0, 0, 0))
    return pl.pallas_call(
        kernel,
        grid=(count,),
        out_shape=[jax.ShapeDtypeStruct((count, size, size), jnp.bfloat16), saved, saved, saved],
        in_specs=[vmem] * (2 * count),
        out_specs=[pl.BlockSpec((1, size, size), lambda i: (i, 0, 0))] + [saved_spec] * 3,
        scratch_shapes=[pltpu.VMEM((size, size), jnp.float32)],
        name="unitary_forward",
    )(*inner_grads, *weights)


def unitary_backward(inner_grads, outer_grads, saved):
    size = inner_grads[0].shape[0]
    count = len(inner_grads)

    def kernel(*refs):
        matrices, outers = refs[:count], refs[count : 2 * count]
        narrow_ref, gram_ref, poly_ref, cot_ref, grad = refs[2 * count :]
        for which in range(count):

            @pl.when(pl.program_id(0) == which)
            def _(which=which):
                grad[...] = -inner_step * outers[which][...]

        def step(back_iteration, carry):
            iteration = NS_STEPS - 1 - back_iteration
            narrow = narrow_ref[0, iteration]
            gram_low = gram_ref[0, iteration]
            grad_low = grad[...].astype(jnp.bfloat16)
            poly_grad = mxu(grad_low, narrow, 1, 1).astype(jnp.bfloat16).astype(jnp.float32)
            pair = poly_grad + poly_grad.T
            product = mxu(pair.astype(jnp.bfloat16), gram_low, 1, 0)
            gram_grad = coef_second * pair + coef_third * (product + product.T)
            narrow_grad = mxu(poly_ref[0, iteration], grad_low, 0, 0) + mxu(
                gram_grad.astype(jnp.bfloat16), narrow, 1, 0
            )
            grad[...] = coef_first * grad[...] + narrow_grad.astype(jnp.bfloat16).astype(
                jnp.float32
            )
            return carry

        lax.fori_loop(0, NS_STEPS, step, 0)
        for which in range(count):

            @pl.when(pl.program_id(0) == which)
            def _(which=which):
                matrix = matrices[which][...]
                inverse = lax.rsqrt(jnp.sum(matrix * matrix) + 1e-06)
                along = jnp.sum(matrix * grad[...]) * inverse * inverse * inverse
                cot_ref[0] = (grad[...] * inverse - matrix * along).astype(jnp.bfloat16)

    vmem = pl.BlockSpec(memory_space=pltpu.VMEM)
    saved_spec = pl.BlockSpec((1, NS_STEPS, size, size), lambda i: (i, 0, 0, 0))
    return pl.pallas_call(
        kernel,
        grid=(count,),
        out_shape=jax.ShapeDtypeStruct((count, size, size), jnp.bfloat16),
        in_specs=[vmem] * (2 * count) + [saved_spec] * 3,
        out_specs=pl.BlockSpec((1, size, size), lambda i: (i, 0, 0)),
        scratch_shapes=[pltpu.VMEM((size, size), jnp.float32)],
        name="unitary_backward",
    )(*inner_grads, *outer_grads, *saved)


def on_core(kernel, name, outs, *operands):
    vmem = pl.BlockSpec(memory_space=pltpu.VMEM)
    return pl.pallas_call(
        kernel,
        out_shape=[jax.ShapeDtypeStruct(shape, kind) for shape, kind in outs],
        in_specs=[vmem] * len(operands),
        out_specs=[vmem] * len(outs),
        name=name,
    )(*operands)


def key_forward(w_gate, w_up, w_down, key_rows, value_rows, step_rates):
    def kernel(gate_w, up_w, down_w, keys, values, rates, a, b, c, gate, up, mid, mixed, target, dgate, dup):
        rows = keys[...]
        key_gate = mxu(rows, gate_w[...], 1, 0)
        key_up = mxu(rows, up_w[...], 1, 0)
        aim = (-rates[...] * values[...].astype(jnp.float32)).astype(jnp.bfloat16)
        key_mid = mxu(aim, down_w[...], 1, 1)
        act_gate, slope_gate, _ = silu_parts(key_gate)
        gate[...] = key_gate
        up[...] = key_up
        mid[...] = key_mid
        target[...] = aim
        mixed[...] = (act_gate * key_up).astype(jnp.bfloat16)
        dgate[...] = (key_mid * key_up * slope_gate).astype(jnp.bfloat16)
        dup[...] = (key_mid * act_gate).astype(jnp.bfloat16)
        a[...] = mxu(rows, dgate[...], 0, 0)
        b[...] = mxu(rows, dup[...], 0, 0)
        c[...] = mxu(mixed[...], target[...], 0, 0)

    square = (w_gate.shape, jnp.float32)
    wide, narrow = (key_rows.shape, jnp.float32), (key_rows.shape, jnp.bfloat16)
    results = on_core(
        kernel,
        "key_forward",
        [square] * 3 + [wide] * 3 + [narrow] * 4,
        w_gate,
        w_up,
        w_down,
        key_rows,
        value_rows,
        step_rates[:, None],
    )
    return results[:3], results[3:]


def key_backward(w_gate, w_up, w_down, key_rows, step_rates, stored, cots):
    def kernel(
        gate_w, up_w, down_w, keys, rates, gate, up, mid, mixed, target, dgate, dup, cots,
        key_grad, value_grad, a, b, c, mid_low, gate_low, up_low,
    ):
        rows = keys[...]
        back_gate = mxu(rows, cots[0], 1, 0)
        back_up = mxu(rows, cots[1], 1, 0)
        back_mixed = mxu(target[...], cots[2], 1, 1)
        key_gate, key_up, key_mid = gate[...], up[...], mid[...]
        act_gate, slope_gate, sigma_gate = silu_parts(key_gate)
        curve_gate = (
            sigma_gate * (1.0 - sigma_gate) * (2.0 + key_gate * (1.0 - 2.0 * sigma_gate))
        )
        mid_low[...] = (back_gate * key_up * slope_gate + back_up * act_gate).astype(jnp.bfloat16)
        gate_low[...] = (
            back_gate * key_mid * key_up * curve_gate
            + back_up * key_mid * slope_gate
            + back_mixed * key_up * slope_gate
        ).astype(jnp.bfloat16)
        up_low[...] = (back_gate * key_mid * slope_gate + back_mixed * act_gate).astype(
            jnp.bfloat16
        )
        a[...] = mxu(rows, gate_low[...], 0, 0)
        b[...] = mxu(rows, up_low[...], 0, 0)
        c[...] = mxu(mid_low[...], target[...], 0, 0)
        key_grad[...] = (
            mxu(dgate[...], cots[0], 1, 1)
            + mxu(dup[...], cots[1], 1, 1)
            + mxu(gate_low[...], gate_w[...], 1, 1)
            + mxu(up_low[...], up_w[...], 1, 1)
        ).astype(jnp.bfloat16)
        value_sum = mxu(mixed[...], cots[2], 1, 0) + mxu(mid_low[...], down_w[...], 1, 0)
        value_grad[...] = (-rates[...] * value_sum).astype(jnp.bfloat16)

    square = (w_gate.shape, jnp.float32)
    narrow = (key_rows.shape, jnp.bfloat16)
    results = on_core(
        kernel,
        "key_backward",
        [narrow] * 2 + [square] * 3 + [narrow] * 3,
        w_gate,
        w_up,
        w_down,
        key_rows,
        step_rates[:, None],
        *stored,
        cots,
    )
    return results[0], results[1], results[2:5]


def query_forward(news, queries, out_gain, cotangent):
    def kernel(news, rows, gain, cot, sums, gate, up, mixed, output):
        query_gate = mxu(rows[...], news[0], 1, 0)
        query_up = mxu(rows[...], news[1], 1, 0)
        gate[...] = query_gate
        up[...] = query_up
        act_gate, _, _ = silu_parts(query_gate)
        mixed[...] = (act_gate * query_up).astype(jnp.bfloat16)
        out = mxu(mixed[...], news[2], 1, 0)
        output[...] = out
        squares = jnp.sum(out * out, axis=1, keepdims=True)
        aligned = jnp.sum(cot[...].astype(jnp.float32) * gain[...] * out, axis=1, keepdims=True)
        lane = lax.broadcasted_iota(jnp.int32, sums.shape, 1)
        sums[...] = jnp.where(lane < sums.shape[1] // 2, squares, aligned)

    wide, narrow = (queries.shape, jnp.float32), (queries.shape, jnp.bfloat16)
    results = on_core(
        kernel,
        "query_forward",
        [((queries.shape[0], 128), jnp.float32), wide, wide, narrow, wide],
        news,
        queries,
        out_gain,
        cotangent,
    )
    return results[0], results[1:]


def query_backward(news, queries, out_gain, cotangent, sums, stored, full_width):
    def kernel(news, rows, gain, cot, sums, gate, up, mixed, output, query_grad, a, b, c, grad, dgate, dup):
        squares = sums[:, :1]
        aligned = sums[:, sums.shape[1] // 2 : sums.shape[1] // 2 + 1]
        inverse_rms = lax.rsqrt(squares / full_width + 1e-05)
        pull = aligned * inverse_rms * inverse_rms * inverse_rms / full_width
        grad[...] = (
            gain[...] * cot[...].astype(jnp.float32) * inverse_rms - output[...] * pull
        ).astype(jnp.bfloat16)
        query_mid = mxu(grad[...], news[2], 1, 1)
        act_gate, slope_gate, _ = silu_parts(gate[...])
        dgate[...] = (query_mid * up[...] * slope_gate).astype(jnp.bfloat16)
        dup[...] = (query_mid * act_gate).astype(jnp.bfloat16)
        a[...] = mxu(rows[...], dgate[...], 0, 0)
        b[...] = mxu(rows[...], dup[...], 0, 0)
        c[...] = mxu(mixed[...], grad[...], 0, 0)
        query_grad[...] = (
            mxu(dgate[...], news[0], 1, 1) + mxu(dup[...], news[1], 1, 1)
        ).astype(jnp.bfloat16)

    square = (news.shape[1:], jnp.float32)
    narrow = (queries.shape, jnp.bfloat16)
    results = on_core(
        kernel,
        "query_backward",
        [narrow] + [square] * 3 + [narrow] * 3,
        news,
        queries,
        out_gain,
        cotangent,
        sums,
        *stored,
    )
    return results[0], results[1:4]


def sum_over_pair(partial, devices, call_id):
    others = devices - 1

    def kernel(given, total, landing, send_sems, recv_sems):
        me = lax.axis_index("head")
        peers = [lax.rem(me + step + 1, devices) for step in range(others)]
        barrier = pltpu.get_barrier_semaphore()
        for peer in peers:
            pl.semaphore_signal(
                barrier, inc=1, device_id={"head": peer}, device_id_type=pl.DeviceIdType.MESH
            )
        pl.semaphore_wait(barrier, others)
        copies = []
        for step, peer in enumerate(peers):
            copy = pltpu.make_async_remote_copy(
                src_ref=given,
                dst_ref=landing.at[step],
                send_sem=send_sems.at[step],
                recv_sem=recv_sems.at[step],
                device_id={"head": peer},
                device_id_type=pl.DeviceIdType.MESH,
            )
            copy.start()
            copies.append(copy)
        result = given[...]
        for step, copy in enumerate(copies):
            copy.wait_recv()
            result = result + landing[step]
        total[...] = result
        for copy in copies:
            copy.wait_send()

    vmem = pl.BlockSpec(memory_space=pltpu.VMEM)
    return pl.pallas_call(
        kernel,
        out_shape=jax.ShapeDtypeStruct(partial.shape, jnp.float32),
        in_specs=[vmem],
        out_specs=vmem,
        scratch_shapes=[pltpu.VMEM((others,) + partial.shape, jnp.float32)]
        + [pltpu.SemaphoreType.DMA((others,))] * 2,
        compiler_params=pltpu.CompilerParams(collective_id=call_id, has_side_effects=True),
        name="sum_pair",
    )(partial)


def bit_orders(bits):
    plain = tuple(range(bits))
    if bits < 3:
        return (plain, plain[::-1])
    if bits == 4:
        return (plain, (0, 2, 1, 3), (1, 0, 3, 2), (1, 3, 0, 2), (2, 0, 1, 3), (3, 1, 0, 2))
    return tuple(plain[turn:] + plain[:turn] for turn in range(bits))


def sum_over_tok(arrays, devices, call_id, whole, added=()):
    bits = devices.bit_length() - 1
    rows, columns = arrays[0].shape
    block = rows // devices
    width = 128
    count = len(arrays)
    orders = bit_orders(bits)
    streams = [
        (array, pl.ds(start, width))
        for array in range(count)
        for start in range(0, columns, width)
    ]
    split = (2,) * bits + (block,)

    def kernel(*refs):
        given = refs[:count]
        addends = refs[count : count + len(added)]
        position = count + len(added)
        shares = refs[position : position + count]
        position += count
        wholes = refs[position : position + count] if whole else ()
        position += len(wholes)
        partial = refs[position : position + count]
        landing = refs[position + count : position + count + bits]
        sems = refs[position + count + bits :]
        me = lax.axis_index("tok")
        mine = [lax.rem(lax.div(me, 1 << bit), 2) for bit in range(bits)]
        partner = [me + (1 - 2 * mine[bit]) * (1 << bit) for bit in range(bits)]

        barrier = pltpu.get_barrier_semaphore()
        for bit in range(bits):
            pl.semaphore_signal(
                barrier,
                inc=1,
                device_id={"tok": partner[bit]},
                device_id_type=pl.DeviceIdType.MESH,
            )
        pl.semaphore_wait(barrier, bits)

        def pick(fixed, lanes):
            leading = tuple(fixed.get(bit, slice(None)) for bit in reversed(range(bits)))
            return leading + (slice(None), lanes)

        sent = []

        def send(source, target, stream, stage, phase, bit):
            copy = pltpu.make_async_remote_copy(
                src_ref=source,
                dst_ref=target,
                send_sem=sems[2 * phase].at[stream, stage],
                recv_sem=sems[2 * phase + 1].at[stream, stage],
                device_id={"tok": partner[bit]},
                device_id_type=pl.DeviceIdType.MESH,
            )
            copy.start()
            sent.append(copy)
            return copy

        def halve(stream, stage):
            array, lanes = streams[stream]
            order = orders[stream % len(orders)]
            fixed = {bit: mine[bit] for bit in order[:stage]}
            bit = order[stage]
            fixed[bit] = 1 - mine[bit]
            held = given[array] if stage == 0 else partial[array]
            return send(
                held.at[pick(fixed, lanes)], landing[stage].at[stream], stream, stage, 0, bit
            )

        def double(stream, stage):
            array, lanes = streams[stream]
            order = orders[stream % len(orders)]
            region = wholes[array].at[pick({bit: mine[bit] for bit in order[: stage + 1]}, lanes)]
            return send(region, region, stream, stage, 1, order[stage])

        flying = {}

        def advance(stream, step):
            array, lanes = streams[stream]
            order = orders[stream % len(orders)]
            if step > 0:
                flying[stream].wait_recv()
            if 0 < step <= bits:
                stage = step - 1
                kept = pick({bit: mine[bit] for bit in order[:step]}, lanes)
                held = given[array] if stage == 0 else partial[array]
                total = held[kept] + landing[stage][stream]
                if step < bits:
                    partial[array][kept] = total
                else:
                    shares[array][:, lanes] = total + addends[array][:, lanes] if added else total
                    if whole:
                        wholes[array][kept] = total
            if step < bits:
                flying[stream] = halve(stream, step)
            elif step < steps:
                flying[stream] = double(stream, 2 * bits - 1 - step)

        steps = 2 * bits if whole else bits
        waves = [range(first, min(first + WAVE, len(streams))) for first in range(0, len(streams), WAVE)]
        begins = [max(0, wave - AHEAD) for wave in range(len(waves))]
        for tick in range(begins[-1] + steps + 1):
            for begin, wave in zip(begins, waves):
                if 0 <= tick - begin <= steps:
                    for stream in wave:
                        advance(stream, tick - begin)
        for copy in sent:
            copy.wait_send()

    phases = 2 if whole else 1
    outs = [jax.ShapeDtypeStruct((block, columns), jnp.float32)] * count
    if whole:
        outs += [jax.ShapeDtypeStruct(split + (columns,), jnp.float32)] * count
    vmem = pl.BlockSpec(memory_space=pltpu.VMEM)
    results = pl.pallas_call(
        kernel,
        out_shape=outs,
        in_specs=[vmem] * (count + len(added)),
        out_specs=[vmem] * len(outs),
        scratch_shapes=[pltpu.VMEM(split + (columns,), jnp.float32)] * count
        + [
            pltpu.VMEM((len(streams),) + (2,) * (bits - 1 - stage) + (block, width), jnp.float32)
            for stage in range(bits)
        ]
        + [pltpu.SemaphoreType.DMA((len(streams), bits))] * (2 * phases),
        compiler_params=pltpu.CompilerParams(collective_id=call_id, has_side_effects=True),
        name="sum_whole" if whole else "sum_share",
    )(*[array.reshape(split + (columns,)) for array in arrays], *added)
    shares = results[:count]
    return shares, [array.reshape(rows, columns) for array in results[count:]]


def local(queries, key_rows, value_rows, step_rates, w_gate, w_up, w_down, out_gain, cotangent):
    heads_here, _, head_size = queries.shape
    assert heads_here == 1
    queries, key_rows, value_rows, step_rates, w_gate, w_up, w_down, cotangent = (
        array[0]
        for array in (
            queries, key_rows, value_rows, step_rates, w_gate, w_up, w_down, cotangent,
        )
    )
    devices = lax.axis_size("tok")
    full_width = lax.axis_size("head") * head_size
    local_grads, stored = key_forward(w_gate, w_up, w_down, key_rows, value_rows, step_rates)
    inner_grads = sum_over_tok(local_grads, devices, 0, True)[1]
    news, *saved = unitary_forward(inner_grads, (w_gate, w_up, w_down))
    sums, query_stored = query_forward(news, queries, out_gain, cotangent)
    sums = sum_over_pair(sums, lax.axis_size("head"), 3)
    query_grad, query_terms = query_backward(
        news, queries, out_gain, cotangent, sums, query_stored, full_width
    )
    query_shares, outer_grads = sum_over_tok(query_terms, devices, 1, True)
    cots = unitary_backward(inner_grads, outer_grads, saved)
    key_grad, value_grad, key_terms = key_backward(
        w_gate, w_up, w_down, key_rows, step_rates, stored, cots
    )
    weight_shares, _ = sum_over_tok(key_terms, devices, 2, False, query_shares)
    return (query_grad[None], key_grad[None], value_grad[None]) + tuple(
        share[None] for share in weight_shares
    )


def solution(mesh):
    in_specs = (
        P("head", "tok", None),
        P("head", "tok", None),
        P("head", "tok", None),
        P("head", "tok"),
        P("head", None, None),
        P("head", None, None),
        P("head", None, None),
        P("head", None),
        P("head", "tok", None),
    )
    out_specs = (
        P("head", "tok", None),
        P("head", "tok", None),
        P("head", "tok", None),
        P("head", "tok", None),
        P("head", "tok", None),
        P("head", "tok", None),
    )
    return jax.shard_map(local, mesh=mesh, in_specs=in_specs, out_specs=out_specs, check_vma=False)
```

```python
import jax
import jax.numpy as jnp
from jax import lax
from jax.experimental import pallas as pl
from jax.experimental.pallas import tpu as pltpu
from jax.sharding import PartitionSpec as P

NS_STEPS = 3
WAVE = 12
AHEAD = 0


coef_first = 3.4445
coef_second = -4.775
coef_third = 2.0315
inner_step = 0.5


def silu_parts(pre_gate):
    sigma_gate = jax.nn.sigmoid(pre_gate)
    act_gate = pre_gate * sigma_gate
    slope_gate = sigma_gate * (1.0 + pre_gate * (1.0 - sigma_gate))
    return (act_gate, slope_gate, sigma_gate)


def mxu(first_op, second_op, first_dim, second_dim):
    return lax.dot_general(
        first_op,
        second_op,
        (((first_dim,), (second_dim,)), ((), ())),
        preferred_element_type=jnp.float32,
    )


def unitary_forward(inner_grads, weights):
    size = weights[0].shape[0]
    count = len(weights)
    every = range(count)

    def kernel(*refs):
        matrices, olds = refs[:count], refs[count : 2 * count]
        new_ref, narrow_ref, gram_ref, poly_ref = refs[2 * count : 2 * count + 4]
        current = refs[2 * count + 4 :]
        for which in every:
            matrix = matrices[which][...]
            current[which][...] = matrix / jnp.sqrt(jnp.sum(matrix * matrix) + 1e-06)

        def step(iteration, carry):
            grams = []
            for which in every:
                narrow = current[which][...].astype(jnp.bfloat16)
                narrow_ref[which, iteration] = narrow
                grams.append(mxu(narrow, narrow, 1, 1))
            for which in every:
                gram_low = grams[which].astype(jnp.bfloat16)
                gram_ref[which, iteration] = gram_low
                poly_ref[which, iteration] = (
                    coef_second * grams[which] + coef_third * mxu(gram_low, gram_low, 1, 0)
                ).astype(jnp.bfloat16)
            for which in every:
                current[which][...] = coef_first * current[which][...] + mxu(
                    poly_ref[which, iteration], narrow_ref[which, iteration], 1, 0
                )
            return carry

        lax.fori_loop(0, NS_STEPS, step, 0)
        for which in every:
            old = olds[which][...].astype(jnp.float32)
            new_ref[which] = (old - inner_step * current[which][...]).astype(jnp.bfloat16)

    saved = ((count, NS_STEPS, size, size), jnp.bfloat16)
    return on_core(
        kernel,
        "unitary_forward",
        [((count, size, size), jnp.bfloat16), saved, saved, saved],
        *inner_grads,
        *weights,
        scratch=[pltpu.VMEM((size, size), jnp.float32)] * count,
    )


def unitary_backward(inner_grads, outer_grads, saved):
    size = inner_grads[0].shape[0]
    count = len(inner_grads)
    every = range(count)

    def kernel(*refs):
        matrices, outers = refs[:count], refs[count : 2 * count]
        narrow_ref, gram_ref, poly_ref, cot_ref = refs[2 * count : 2 * count + 4]
        grad = refs[2 * count + 4 :]
        for which in every:
            grad[which][...] = -inner_step * outers[which][...]

        def step(back_iteration, carry):
            iteration = NS_STEPS - 1 - back_iteration
            pairs = []
            for which in every:
                poly_grad = mxu(
                    grad[which][...].astype(jnp.bfloat16), narrow_ref[which, iteration], 1, 1
                )
                poly_grad = poly_grad.astype(jnp.bfloat16).astype(jnp.float32)
                pairs.append(poly_grad + poly_grad.T)
            for which in every:
                pair = pairs[which]
                product = mxu(pair.astype(jnp.bfloat16), gram_ref[which, iteration], 1, 0)
                pairs[which] = (
                    coef_second * pair + coef_third * (product + product.T)
                ).astype(jnp.bfloat16)
            for which in every:
                grad_low = grad[which][...].astype(jnp.bfloat16)
                narrow_grad = mxu(poly_ref[which, iteration], grad_low, 1, 0) + mxu(
                    pairs[which], narrow_ref[which, iteration], 1, 0
                )
                grad[which][...] = coef_first * grad[which][...] + narrow_grad.astype(
                    jnp.bfloat16
                ).astype(jnp.float32)
            return carry

        lax.fori_loop(0, NS_STEPS, step, 0)
        for which in every:
            matrix = matrices[which][...]
            inverse = lax.rsqrt(jnp.sum(matrix * matrix) + 1e-06)
            along = jnp.sum(matrix * grad[which][...]) * inverse * inverse * inverse
            cot_ref[which] = (grad[which][...] * inverse - matrix * along).astype(jnp.bfloat16)

    return on_core(
        kernel,
        "unitary_backward",
        [((count, size, size), jnp.bfloat16)],
        *inner_grads,
        *outer_grads,
        *saved,
        scratch=[pltpu.VMEM((size, size), jnp.float32)] * count,
    )[0]


def on_core(kernel, name, outs, *operands, scratch=()):
    vmem = pl.BlockSpec(memory_space=pltpu.VMEM)
    return pl.pallas_call(
        kernel,
        out_shape=[jax.ShapeDtypeStruct(shape, kind) for shape, kind in outs],
        in_specs=[vmem] * len(operands),
        out_specs=[vmem] * len(outs),
        scratch_shapes=list(scratch),
        name=name,
    )(*operands)


def column_of(row):
    return jnp.broadcast_to(row, (128, row.shape[1])).T[:, :1]


def key_forward(w_gate, w_up, w_down, key_rows, value_rows, step_rates):
    def kernel(gate_w, up_w, down_w, keys, values, rates, a, b, c, gate, up, mid, mixed, target, dgate, dup):
        rows = keys[...]
        key_gate = mxu(rows, gate_w[...], 1, 0)
        key_up = mxu(rows, up_w[...], 1, 0)
        aim = (-column_of(rates[...]) * values[...].astype(jnp.float32)).astype(jnp.bfloat16)
        key_mid = mxu(aim, down_w[...], 1, 1)
        act_gate, slope_gate, _ = silu_parts(key_gate)
        gate[...] = key_gate
        up[...] = key_up
        mid[...] = key_mid
        target[...] = aim
        mixed[...] = (act_gate * key_up).astype(jnp.bfloat16)
        dgate[...] = (key_mid * key_up * slope_gate).astype(jnp.bfloat16)
        dup[...] = (key_mid * act_gate).astype(jnp.bfloat16)
        a[...] = mxu(rows, dgate[...], 0, 0)
        b[...] = mxu(rows, dup[...], 0, 0)
        c[...] = mxu(mixed[...], target[...], 0, 0)

    square = (w_gate.shape, jnp.float32)
    wide, narrow = (key_rows.shape, jnp.float32), (key_rows.shape, jnp.bfloat16)
    results = on_core(
        kernel,
        "key_forward",
        [square] * 3 + [wide] * 3 + [narrow] * 4,
        w_gate,
        w_up,
        w_down,
        key_rows,
        value_rows,
        step_rates[None],
    )
    return results[:3], results[3:]


def key_backward(w_gate, w_up, w_down, key_rows, step_rates, stored, cots):
    def kernel(
        gate_w, up_w, down_w, keys, rates, gate, up, mid, mixed, target, dgate, dup, cots,
        key_grad, value_grad, a, b, c, mid_low, gate_low, up_low,
    ):
        rows = keys[...]
        back_gate = mxu(rows, cots[0], 1, 0)
        back_up = mxu(rows, cots[1], 1, 0)
        back_mixed = mxu(target[...], cots[2], 1, 1)
        key_gate, key_up, key_mid = gate[...], up[...], mid[...]
        act_gate, slope_gate, sigma_gate = silu_parts(key_gate)
        curve_gate = (
            sigma_gate * (1.0 - sigma_gate) * (2.0 + key_gate * (1.0 - 2.0 * sigma_gate))
        )
        mid_low[...] = (back_gate * key_up * slope_gate + back_up * act_gate).astype(jnp.bfloat16)
        gate_low[...] = (
            back_gate * key_mid * key_up * curve_gate
            + back_up * key_mid * slope_gate
            + back_mixed * key_up * slope_gate
        ).astype(jnp.bfloat16)
        up_low[...] = (back_gate * key_mid * slope_gate + back_mixed * act_gate).astype(
            jnp.bfloat16
        )
        a[...] = mxu(rows, gate_low[...], 0, 0)
        b[...] = mxu(rows, up_low[...], 0, 0)
        c[...] = mxu(mid_low[...], target[...], 0, 0)
        key_grad[...] = (
            mxu(dgate[...], cots[0], 1, 1)
            + mxu(dup[...], cots[1], 1, 1)
            + mxu(gate_low[...], gate_w[...], 1, 1)
            + mxu(up_low[...], up_w[...], 1, 1)
        ).astype(jnp.bfloat16)
        value_sum = mxu(mixed[...], cots[2], 1, 0) + mxu(mid_low[...], down_w[...], 1, 0)
        value_grad[...] = (-column_of(rates[...]) * value_sum).astype(jnp.bfloat16)

    square = (w_gate.shape, jnp.float32)
    narrow = (key_rows.shape, jnp.bfloat16)
    results = on_core(
        kernel,
        "key_backward",
        [narrow] * 2 + [square] * 3 + [narrow] * 3,
        w_gate,
        w_up,
        w_down,
        key_rows,
        step_rates[None],
        *stored,
        cots,
    )
    return results[0], results[1], results[2:5]


def add_shares(first, second):
    count = len(first)

    def kernel(*refs):
        for which in range(count):
            refs[2 * count + which][...] = refs[which][...] + refs[count + which][...]

    return on_core(
        kernel, "add_shares", [(share.shape, jnp.float32) for share in first], *first, *second
    )


def query_forward(news, queries, out_gain, cotangent):
    def kernel(news, rows, gain, cot, sums, gate, up, mixed, output):
        query_gate = mxu(rows[...], news[0], 1, 0)
        query_up = mxu(rows[...], news[1], 1, 0)
        gate[...] = query_gate
        up[...] = query_up
        act_gate, _, _ = silu_parts(query_gate)
        mixed[...] = (act_gate * query_up).astype(jnp.bfloat16)
        out = mxu(mixed[...], news[2], 1, 0)
        output[...] = out
        squares = jnp.sum(out * out, axis=1, keepdims=True)
        aligned = jnp.sum(cot[...].astype(jnp.float32) * gain[...] * out, axis=1, keepdims=True)
        lane = lax.broadcasted_iota(jnp.int32, sums.shape, 1)
        sums[...] = jnp.where(lane < sums.shape[1] // 2, squares, aligned)

    wide, narrow = (queries.shape, jnp.float32), (queries.shape, jnp.bfloat16)
    results = on_core(
        kernel,
        "query_forward",
        [((queries.shape[0], 128), jnp.float32), wide, wide, narrow, wide],
        news,
        queries,
        out_gain,
        cotangent,
    )
    return results[0], results[1:]


def query_backward(news, queries, out_gain, cotangent, sums, stored, full_width):
    def kernel(news, rows, gain, cot, sums, gate, up, mixed, output, query_grad, a, b, c, grad, dgate, dup):
        squares = sums[:, :1]
        aligned = sums[:, sums.shape[1] // 2 : sums.shape[1] // 2 + 1]
        inverse_rms = lax.rsqrt(squares / full_width + 1e-05)
        pull = aligned * inverse_rms * inverse_rms * inverse_rms / full_width
        grad[...] = (
            gain[...] * cot[...].astype(jnp.float32) * inverse_rms - output[...] * pull
        ).astype(jnp.bfloat16)
        query_mid = mxu(grad[...], news[2], 1, 1)
        act_gate, slope_gate, _ = silu_parts(gate[...])
        dgate[...] = (query_mid * up[...] * slope_gate).astype(jnp.bfloat16)
        dup[...] = (query_mid * act_gate).astype(jnp.bfloat16)
        a[...] = mxu(rows[...], dgate[...], 0, 0)
        b[...] = mxu(rows[...], dup[...], 0, 0)
        c[...] = mxu(mixed[...], grad[...], 0, 0)
        query_grad[...] = (
            mxu(dgate[...], news[0], 1, 1) + mxu(dup[...], news[1], 1, 1)
        ).astype(jnp.bfloat16)

    square = (news.shape[1:], jnp.float32)
    narrow = (queries.shape, jnp.bfloat16)
    results = on_core(
        kernel,
        "query_backward",
        [narrow] + [square] * 3 + [narrow] * 3,
        news,
        queries,
        out_gain,
        cotangent,
        sums,
        *stored,
    )
    return results[0], results[1:4]


def sum_over_pair(partial, devices, call_id):
    others = devices - 1

    def kernel(given, total, landing, send_sems, recv_sems):
        me = lax.axis_index("head")
        peers = [lax.rem(me + step + 1, devices) for step in range(others)]
        barrier = pltpu.get_barrier_semaphore()
        for peer in peers:
            pl.semaphore_signal(
                barrier, inc=1, device_id={"head": peer}, device_id_type=pl.DeviceIdType.MESH
            )
        pl.semaphore_wait(barrier, others)
        copies = []
        for step, peer in enumerate(peers):
            copy = pltpu.make_async_remote_copy(
                src_ref=given,
                dst_ref=landing.at[step],
                send_sem=send_sems.at[step],
                recv_sem=recv_sems.at[step],
                device_id={"head": peer},
                device_id_type=pl.DeviceIdType.MESH,
            )
            copy.start()
            copies.append(copy)
        result = given[...]
        for step, copy in enumerate(copies):
            copy.wait_recv()
            result = result + landing[step]
        total[...] = result
        for copy in copies:
            copy.wait_send()

    vmem = pl.BlockSpec(memory_space=pltpu.VMEM)
    return pl.pallas_call(
        kernel,
        out_shape=jax.ShapeDtypeStruct(partial.shape, jnp.float32),
        in_specs=[vmem],
        out_specs=vmem,
        scratch_shapes=[pltpu.VMEM((others,) + partial.shape, jnp.float32)]
        + [pltpu.SemaphoreType.DMA((others,))] * 2,
        compiler_params=pltpu.CompilerParams(collective_id=call_id, has_side_effects=True),
        name="sum_pair",
    )(partial)


def bit_orders(bits):
    plain = tuple(range(bits))
    if bits < 3:
        return (plain, plain[::-1])
    if bits == 4:
        return (plain, (0, 2, 1, 3), (1, 0, 3, 2), (1, 3, 0, 2), (2, 0, 1, 3), (3, 1, 0, 2))
    return tuple(plain[turn:] + plain[:turn] for turn in range(bits))


def sum_over_tok(arrays, devices, call_id, whole):
    bits = devices.bit_length() - 1
    rows, columns = arrays[0].shape
    block = rows // devices
    width = 128
    count = len(arrays)
    orders = bit_orders(bits)
    streams = [
        (array, pl.ds(start, width))
        for array in range(count)
        for start in range(0, columns, width)
    ]
    split = (2,) * bits + (block,)

    def kernel(*refs):
        given = refs[:count]
        shares = refs[count : 2 * count]
        position = 2 * count
        wholes = refs[position : position + count] if whole else ()
        position += len(wholes)
        partial = refs[position : position + count]
        landing = refs[position + count : position + count + bits]
        sems = refs[position + count + bits :]
        me = lax.axis_index("tok")
        mine = [lax.rem(lax.div(me, 1 << bit), 2) for bit in range(bits)]
        partner = [me + (1 - 2 * mine[bit]) * (1 << bit) for bit in range(bits)]

        barrier = pltpu.get_barrier_semaphore()
        for bit in range(bits):
            pl.semaphore_signal(
                barrier,
                inc=1,
                device_id={"tok": partner[bit]},
                device_id_type=pl.DeviceIdType.MESH,
            )
        pl.semaphore_wait(barrier, bits)

        def pick(fixed, lanes):
            leading = tuple(fixed.get(bit, slice(None)) for bit in reversed(range(bits)))
            return leading + (slice(None), lanes)

        sent = []

        def send(source, target, stream, stage, phase, bit):
            copy = pltpu.make_async_remote_copy(
                src_ref=source,
                dst_ref=target,
                send_sem=sems[2 * phase].at[stream, stage],
                recv_sem=sems[2 * phase + 1].at[stream, stage],
                device_id={"tok": partner[bit]},
                device_id_type=pl.DeviceIdType.MESH,
            )
            copy.start()
            sent.append(copy)
            return copy

        def halve(stream, stage):
            array, lanes = streams[stream]
            order = orders[stream % len(orders)]
            fixed = {bit: mine[bit] for bit in order[:stage]}
            bit = order[stage]
            fixed[bit] = 1 - mine[bit]
            held = given[array] if stage == 0 else partial[array]
            return send(
                held.at[pick(fixed, lanes)], landing[stage].at[stream], stream, stage, 0, bit
            )

        def double(stream, stage):
            array, lanes = streams[stream]
            order = orders[stream % len(orders)]
            region = wholes[array].at[pick({bit: mine[bit] for bit in order[: stage + 1]}, lanes)]
            return send(region, region, stream, stage, 1, order[stage])

        flying = {}

        def advance(stream, step):
            array, lanes = streams[stream]
            order = orders[stream % len(orders)]
            if step > 0:
                flying[stream].wait_recv()
            if 0 < step <= bits:
                stage = step - 1
                kept = pick({bit: mine[bit] for bit in order[:step]}, lanes)
                held = given[array] if stage == 0 else partial[array]
                total = held[kept] + landing[stage][stream]
                if step < bits:
                    partial[array][kept] = total
                else:
                    shares[array][:, lanes] = total
                    if whole:
                        wholes[array][kept] = total
            if step < bits:
                flying[stream] = halve(stream, step)
            elif step < steps:
                flying[stream] = double(stream, 2 * bits - 1 - step)

        steps = 2 * bits if whole else bits
        waves = [range(first, min(first + WAVE, len(streams))) for first in range(0, len(streams), WAVE)]
        begins = [max(0, wave - AHEAD) for wave in range(len(waves))]
        for tick in range(begins[-1] + steps + 1):
            for begin, wave in zip(begins, waves):
                if 0 <= tick - begin <= steps:
                    for stream in wave:
                        advance(stream, tick - begin)
        for copy in sent:
            copy.wait_send()

    phases = 2 if whole else 1
    outs = [jax.ShapeDtypeStruct((block, columns), jnp.float32)] * count
    if whole:
        outs += [jax.ShapeDtypeStruct(split + (columns,), jnp.float32)] * count
    vmem = pl.BlockSpec(memory_space=pltpu.VMEM)
    results = pl.pallas_call(
        kernel,
        out_shape=outs,
        in_specs=[vmem] * count,
        out_specs=[vmem] * len(outs),
        scratch_shapes=[pltpu.VMEM(split + (columns,), jnp.float32)] * count
        + [
            pltpu.VMEM((len(streams),) + (2,) * (bits - 1 - stage) + (block, width), jnp.float32)
            for stage in range(bits)
        ]
        + [pltpu.SemaphoreType.DMA((len(streams), bits))] * (2 * phases),
        compiler_params=pltpu.CompilerParams(collective_id=call_id, has_side_effects=True),
        name="sum_whole" if whole else "sum_share",
    )(*[array.reshape(split + (columns,)) for array in arrays])
    shares = results[:count]
    return shares, [array.reshape(rows, columns) for array in results[count:]]


def local(queries, key_rows, value_rows, step_rates, w_gate, w_up, w_down, out_gain, cotangent):
    heads_here, _, head_size = queries.shape
    assert heads_here == 1
    queries, key_rows, value_rows, step_rates, w_gate, w_up, w_down, cotangent = (
        array[0]
        for array in (
            queries, key_rows, value_rows, step_rates, w_gate, w_up, w_down, cotangent,
        )
    )
    devices = lax.axis_size("tok")
    full_width = lax.axis_size("head") * head_size
    local_grads, stored = key_forward(w_gate, w_up, w_down, key_rows, value_rows, step_rates)
    inner_grads = sum_over_tok(local_grads, devices, 0, True)[1]
    news, *saved = unitary_forward(inner_grads, (w_gate, w_up, w_down))
    sums, query_stored = query_forward(news, queries, out_gain, cotangent)
    sums = sum_over_pair(sums, lax.axis_size("head"), 3)
    query_grad, query_terms = query_backward(
        news, queries, out_gain, cotangent, sums, query_stored, full_width
    )
    query_shares, outer_grads = sum_over_tok(query_terms, devices, 1, True)
    cots = unitary_backward(inner_grads, outer_grads, saved)
    key_grad, value_grad, key_terms = key_backward(
        w_gate, w_up, w_down, key_rows, step_rates, stored, cots
    )
    key_shares, _ = sum_over_tok(key_terms, devices, 2, False)
    weight_shares = add_shares(query_shares, key_shares)
    return (query_grad[None], key_grad[None], value_grad[None]) + tuple(
        share[None] for share in weight_shares
    )


def solution(mesh):
    in_specs = (
        P("head", "tok", None),
        P("head", "tok", None),
        P("head", "tok", None),
        P("head", "tok"),
        P("head", None, None),
        P("head", None, None),
        P("head", None, None),
        P("head", None),
        P("head", "tok", None),
    )
    out_specs = (
        P("head", "tok", None),
        P("head", "tok", None),
        P("head", "tok", None),
        P("head", "tok", None),
        P("head", "tok", None),
        P("head", "tok", None),
    )
    return jax.shard_map(local, mesh=mesh, in_specs=in_specs, out_specs=out_specs, check_vma=False)
```
